32 devices in a mesh: row: 8 (over y, x, core), col: 4 (over z).
Axes of the slice: x: 2, y: 2, z: 4, core: 2. Of those that a mesh axis runs over, the one named last changes fastest.
Arguments:
- coeffs: bfloat16 [6144, 4096], P('row', 'col'), may hold values from -0.00390625 to 0.00390625
- occupation: float32 [4096], P('col'), may hold values from 0.5 to 2
- basis_on_grid: bfloat16 [320, 512, 512], P('row'), may hold values from -6 to 6
- basis_map: int32 [320, 512], P('row'), may hold values from 0 to 6143, as said below
- basis_count: int32 [320], P('row'), may hold values from 256 to 512
- batch_atom: int32 [320], P('row'), may hold values from 0 to 63
- harmonics: float32 [320, 49, 512], P('row'), may hold values from -0.25 to 0.25
Outputs:
- density: float32 [320, 512], P('row', 'col')
- moments: float32 [64, 49], replicated
The draws below stay inside these ranges and needn't reach their ends.
Inputs may be any that keep to these rules, and one draw needn't show every extreme that they name: `basis_map`: the slots of one batch name distinct basis functions. With R = 768 and o = b // 40, batch b names only basis functions q * R + (o * 96 + w) mod R with 0 <= q < 8 and 0 <= w < 96.
All inputs are finite; a program needn't handle non-finite values.
Results may differ from the reference program's by a relative error of at most 0.0003.
Values may be sent and summed in bfloat16 or wider, within the bound.
No kernel may reach another device: no remote copies, remote signals or barrier semaphores. Data moves between devices by JAX's collectives and lax.ppermute only.
A program may use at most 192 MiB of HBM per device.

```python
import jax
import jax.numpy as jnp
from jax import lax

NB = 6144
NOCC = 4096
SLOTS = 512
WIN = 96
POINTS = 512
LM = 49
NATOM = 64
BD = 40
BATCHES = 320


def draw_basis_map(key, part):
    owners = BATCHES // BD
    shard = NB // owners
    keys = jax.random.split(jax.random.fold_in(key, 7), BATCHES)
    chosen = jax.vmap(lambda one: jax.random.permutation(one, WIN * owners))(keys)[:, :SLOTS]
    chosen = chosen.astype(jnp.int32)
    source = chosen // WIN
    offset = chosen % WIN
    owner = jnp.arange(BATCHES, dtype=jnp.int32) // BD
    local = jnp.mod(owner[:, None] * WIN + offset, shard)
    return (source * shard + local).astype(jnp.int32)


def set_ends(values, own_key, low, high):
    longest = values.shape.index(max(values.shape))
    spots = []
    for shift in (0, 1):
        where = [jax.random.randint(jax.random.fold_in(own_key, axis), (), 0, length) for axis, length in enumerate(values.shape)]
        where[longest] = (where[longest] + shift) % values.shape[longest]
        spots.append(tuple(where))
    return values.at[spots[0]].set(low).at[spots[1]].set(high)


def block_scale(own_key, extent, cuts, smallest, largest):
    gain, own = 1.0, jax.random.fold_in(own_key, 6)
    for position, shards_of in cuts:
        heights = jnp.exp(jax.random.uniform(jax.random.fold_in(own, position), (shards_of,), jnp.float32, smallest / len(cuts), largest / len(cuts)))
        gain = gain * jnp.repeat(heights, extent[position] // shards_of).reshape([-1 if axis == position else 1 for axis in range(len(extent))])
    return gain


def centred(rng, extent, deviation, limit, pieces=(), held_as=jnp.bfloat16):
    factor_of = block_scale(rng, extent, pieces, -0.22, 0.18) if pieces else 1.0
    entries = jax.random.normal(rng, extent, jnp.float32) * deviation * factor_of
    return jnp.minimum(jnp.maximum(entries, -limit), limit).astype(held_as)


def setup_inputs(seed: int = 0) -> dict:
    seeds = jax.random.split(jax.random.key(seed), 8)
    return {
        "coeffs": centred(seeds[0], (NB, NOCC), (SLOTS * NOCC) ** -0.5, 0.00390625, ((0, 8), (1, 4))),
        "occupation": jnp.clip(0.5 + 1.5 * jax.random.uniform(seeds[1], (NOCC,), jnp.float32) ** block_scale(seeds[1], (NOCC,), ((0, 4),), -0.2, 0.2), 0.5, 2.0),
        "basis_on_grid": centred(seeds[2], (BATCHES, POINTS, SLOTS), 1.0, 6.0, ((0, 8),)),
        "basis_map": draw_basis_map(jax.random.fold_in(seeds[7], 71), 0),
        "basis_count": set_ends(jax.random.randint(seeds[4], (BATCHES,), SLOTS // 2, SLOTS + 1), jax.random.fold_in(seeds[4], 1), SLOTS // 2, SLOTS).astype(jnp.int32),
        "batch_atom": set_ends(jax.random.randint(seeds[5], (BATCHES,), 0, NATOM), jax.random.fold_in(seeds[5], 1), 0, NATOM - 1).astype(jnp.int32),
        "harmonics": centred(seeds[6], (BATCHES, LM, POINTS), POINTS ** -0.5, 0.25, ((0, 8),), jnp.float32),
    }


def reference(coeffs, occupation, basis_on_grid, basis_map, basis_count, batch_atom, harmonics):
    slot_ids = jnp.arange(SLOTS, dtype=jnp.int32)

    def one_batch(items):
        values, indices, count = items
        selected = jnp.take(coeffs, indices, axis=0)
        keep = slot_ids < count
        masked = jnp.where(keep[None, :], values, jnp.zeros_like(values))
        orbital = jnp.dot(masked, selected, preferred_element_type=jnp.float32)
        return jnp.sum(occupation[None, :] * orbital * orbital, axis=1)

    density = lax.map(one_batch, (basis_on_grid, basis_map, basis_count))
    local_moment = jnp.einsum("blp,bp->bl", harmonics, density, precision=lax.Precision.HIGHEST)
    member = (batch_atom[:, None] == jnp.arange(NATOM, dtype=jnp.int32)[None, :]).astype(jnp.float32)
    moments = jnp.dot(member.T, local_moment, precision=lax.Precision.HIGHEST)
    return density, moments
```

```python
import jax
import jax.numpy as jnp
from jax import lax
from jax.experimental import pallas as pl
from jax.experimental.pallas import tpu as pltpu
from jax.sharding import PartitionSpec as P

WIN = 96
NATOM = 64


def spread_kernel(ids_ref, values_ref, out_ref):
    wide = out_ref.shape[1]
    slots = ids_ref.shape[2]
    rows = lax.broadcasted_iota(jnp.int32, (wide, slots), 0)
    place = jnp.where(rows == ids_ref[0], 1.0, 0.0).astype(jnp.bfloat16)
    out = lax.dot_general(
        place, values_ref[0], (((1,), (1,)), ((), ())), preferred_element_type=jnp.float32
    )
    out_ref[0] = out.astype(jnp.bfloat16)


def spread(ids, values, wide):
    batches, points, slots = values.shape
    return pl.pallas_call(
        spread_kernel,
        grid=(batches,),
        in_specs=[
            pl.BlockSpec((1, 1, slots), lambda b: (b, 0, 0)),
            pl.BlockSpec((1, points, slots), lambda b: (b, 0, 0)),
        ],
        out_specs=pl.BlockSpec((1, wide, points), lambda b: (b, 0, 0)),
        out_shape=jax.ShapeDtypeStruct((batches, wide, points), jnp.bfloat16),
        compiler_params=pltpu.CompilerParams(dimension_semantics=("arbitrary",)),
        cost_estimate=pl.CostEstimate(
            flops=2 * batches * points * slots * wide,
            bytes_accessed=2 * batches * points * (slots + wide),
            transcendentals=0,
        ),
    )(ids[:, None, :], values)


def density_kernel(atom_ref, spread_ref, window_ref, occ_ref, harm_ref, den_ref, mom_ref, turned):
    b = pl.program_id(0)

    @pl.when(b == 0)
    def _():
        turned[...] = window_ref[...].T
        mom_ref[...] = jnp.zeros_like(mom_ref)

    states, _ = turned.shape
    points = spread_ref.shape[2]
    step = min(256, states)
    values = spread_ref[0]
    total = jnp.zeros((8, points), jnp.float32)
    for first in range(0, states, step):
        orbital = jnp.dot(turned[first:first + step, :], values, preferred_element_type=jnp.float32)
        weight = jnp.tile(occ_ref[first:first + step, :], (1, points // occ_ref.shape[1]))
        scaled = orbital * orbital * weight
        total = total + jnp.sum(scaled.reshape(step // 8, 8, points), axis=0)
    density = jnp.sum(total, axis=0, keepdims=True)
    den_ref[0] = density
    local = jnp.sum(harm_ref[0] * density, axis=1, keepdims=True)
    atoms = lax.broadcasted_iota(jnp.int32, mom_ref.shape, 1)
    mom_ref[...] += jnp.where(atoms == atom_ref[b], local, 0.0)


def densities(batch_atom, spreads, window, occupation, harmonics):
    batches, wide, points = spreads.shape
    states = window.shape[1]
    parts = harmonics.shape[1]
    lanes = min(128, points)
    occ = jnp.broadcast_to(occupation[:, None], (states, lanes))
    return pl.pallas_call(
        density_kernel,
        grid_spec=pltpu.PrefetchScalarGridSpec(
            num_scalar_prefetch=1,
            grid=(batches,),
            in_specs=[
                pl.BlockSpec((1, wide, points), lambda b, a: (b, 0, 0)),
                pl.BlockSpec((wide, states), lambda b, a: (0, 0)),
                pl.BlockSpec((states, lanes), lambda b, a: (0, 0)),
                pl.BlockSpec((1, parts, points), lambda b, a: (b, 0, 0)),
            ],
            out_specs=[
                pl.BlockSpec((1, 1, points), lambda b, a: (b, 0, 0)),
                pl.BlockSpec((parts, NATOM), lambda b, a: (0, 0)),
            ],
            scratch_shapes=[pltpu.VMEM((states, wide), jnp.bfloat16)],
        ),
        out_shape=[
            jax.ShapeDtypeStruct((batches, 1, points), jnp.float32),
            jax.ShapeDtypeStruct((parts, NATOM), jnp.float32),
        ],
        compiler_params=pltpu.CompilerParams(dimension_semantics=("arbitrary",)),
        cost_estimate=pl.CostEstimate(
            flops=2 * batches * points * wide * states,
            bytes_accessed=2 * batches * points * wide,
            transcendentals=0,
        ),
    )(batch_atom, spreads, window, occ, harmonics)


def shards(coeffs, occupation, basis_on_grid, basis_map, basis_count, batch_atom, harmonics):
    batches, points, slots = basis_on_grid.shape
    owned = coeffs.shape[0]
    owners = lax.axis_size("row")
    wide = owners * WIN
    if wide == owned:
        outgoing = coeffs
    else:
        target = lax.broadcasted_iota(jnp.int32, (owners, WIN), 0)
        offset = lax.broadcasted_iota(jnp.int32, (owners, WIN), 1)
        outgoing = jnp.take(coeffs, jnp.mod(target * WIN + offset, owned).reshape(-1), axis=0)
    window = lax.all_to_all(outgoing, "row", split_axis=0, concat_axis=0, tiled=True)
    start = jnp.mod(lax.axis_index("row") * WIN, owned)
    source = basis_map // owned
    within = jnp.mod(basis_map % owned - start, owned)
    local_ids = source * WIN + within
    slot_ids = lax.broadcasted_iota(jnp.int32, (batches, slots), 1)
    local_ids = jnp.where(slot_ids < basis_count[:, None], local_ids, -1)
    spreads = spread(local_ids, basis_on_grid, wide)
    partial, atom_part = densities(batch_atom, spreads, window, occupation, harmonics)
    density = lax.psum_scatter(partial[:, 0, :], "col", scatter_dimension=1, tiled=True)
    moments = lax.psum(atom_part, ("row", "col")).T
    return (density, moments)


def solution(mesh):
    placed = (
        P("row", "col"),
        P("col"),
        P("row", None, None),
        P("row", None),
        P("row"),
        P("row"),
        P("row", None, None),
    )
    return jax.shard_map(
        shards, mesh=mesh, in_specs=placed, out_specs=(P("row", "col"), P()), check_vma=False
    )
```

```python
import jax
import jax.numpy as jnp
from jax import lax
from jax.experimental import pallas as pl
from jax.experimental.pallas import tpu as pltpu
from jax.sharding import PartitionSpec as P

WIN = 96
NATOM = 64


GROUP = 8


def spread_kernel(ids_ref, values_ref, out_ref):
    per, points, wide = out_ref.shape
    slots = ids_ref.shape[1]
    columns = lax.broadcasted_iota(jnp.int32, (slots, wide), 1)
    for j in range(per):
        place = jnp.where(columns == ids_ref[0, :, j:j + 1], 1.0, 0.0).astype(jnp.bfloat16)
        out = jnp.dot(values_ref[j], place, preferred_element_type=jnp.float32)
        out_ref[j] = out.astype(jnp.bfloat16)


def spread(ids, values, wide):
    batches, points, slots = values.shape
    per = next(n for n in (4, 2, 1) if batches % n == 0 and n * wide <= 4096)
    ids = ids.reshape(batches // per, per, slots).transpose(0, 2, 1)
    return pl.pallas_call(
        spread_kernel,
        grid=(batches // per,),
        in_specs=[
            pl.BlockSpec((1, slots, per), lambda b: (b, 0, 0)),
            pl.BlockSpec((per, points, slots), lambda b: (b, 0, 0)),
        ],
        out_specs=pl.BlockSpec((per, points, wide), lambda b: (b, 0, 0)),
        out_shape=jax.ShapeDtypeStruct((batches, points, wide), jnp.bfloat16),
        compiler_params=pltpu.CompilerParams(dimension_semantics=("arbitrary",)),
        cost_estimate=pl.CostEstimate(
            flops=2 * batches * points * slots * wide,
            bytes_accessed=2 * batches * points * (slots + wide),
            transcendentals=0,
        ),
    )(ids, values)


def density_kernel(atom_ref, spread_ref, window_ref, occ_ref, harm_ref, out_ref, mom, rows):
    per = spread_ref.shape[0]
    _, points, wide = spread_ref.shape
    states = window_ref.shape[1]
    cols, _, share = out_ref.shape
    parts = harm_ref.shape[0]
    i = pl.program_id(0)
    first = pl.multiple_of(i * per, per)
    inner = lax.rem(first, GROUP)

    @pl.when(i == 0)
    def _():
        mom[...] = jnp.zeros_like(mom)

    step = min(256, states)
    lanes = min(128, step)
    pair = min(2, per)
    for j in range(0, per, pair):
        values = spread_ref[j:j + pair].reshape(pair * points, wide)
        total = jnp.zeros((pair * points, lanes), jnp.float32)
        for start in range(0, states, step):
            orbital = jnp.dot(
                values, window_ref[:, start:start + step], preferred_element_type=jnp.float32
            )
            scaled = orbital * orbital * occ_ref[:, start:start + step]
            for lane in range(0, step, lanes):
                total = total + scaled[:, lane:lane + lanes]
        for k in range(pair):
            piece = total[k * points:(k + 1) * points].T
            rows[pl.ds(inner + j + k, 1), :] = jnp.sum(piece, axis=0, keepdims=True)

    @pl.when(inner + per == GROUP)
    def _():
        base = pl.multiple_of(first + per - GROUP, GROUP)
        density = rows[...]
        for c in range(cols):
            out_ref[c, pl.ds(base, GROUP), :] = density[:, c * share:(c + 1) * share]
        local = jnp.sum(harm_ref[...] * density[None], axis=2, keepdims=True)
        spots = lax.broadcasted_iota(jnp.int32, (GROUP, NATOM), 0)
        atoms = jnp.zeros((GROUP, NATOM), jnp.int32)
        for k in range(GROUP):
            atoms = jnp.where(spots == k, atom_ref[base + k], atoms)
        lanes_of = lax.broadcasted_iota(jnp.int32, (GROUP, NATOM), 1)
        member = jnp.where(atoms == lanes_of, 1.0, 0.0)
        mom[...] += local * member[None]

    @pl.when(i == pl.num_programs(0) - 1)
    def _():
        done = jnp.sum(mom[...], axis=1)
        batches = pl.num_programs(0) * per
        for c in range(cols):
            out_ref[c, pl.ds(batches, parts), :NATOM] = done


def densities(batch_atom, spreads, window, occupation, harmonics, cols):
    batches, points, wide = spreads.shape
    states = window.shape[1]
    parts = harmonics.shape[1]
    share = points // cols
    per = GROUP if wide <= 1024 else 2
    height = batches + -(-parts // GROUP) * GROUP
    ratio = GROUP // per
    return pl.pallas_call(
        density_kernel,
        grid_spec=pltpu.PrefetchScalarGridSpec(
            num_scalar_prefetch=1,
            grid=(batches // per,),
            in_specs=[
                pl.BlockSpec((per, points, wide), lambda b, a: (b, 0, 0)),
                pl.BlockSpec((wide, states), lambda b, a: (0, 0)),
                pl.BlockSpec((1, states), lambda b, a: (0, 0)),
                pl.BlockSpec((parts, GROUP, points), lambda b, a: (0, b // ratio, 0)),
            ],
            out_specs=pl.BlockSpec((cols, height, share), lambda b, a: (0, 0, 0)),
            scratch_shapes=[
                pltpu.VMEM((parts, GROUP, NATOM), jnp.float32),
                pltpu.VMEM((GROUP, points), jnp.float32),
            ],
        ),
        out_shape=jax.ShapeDtypeStruct((cols, height, share), jnp.float32),
        compiler_params=pltpu.CompilerParams(dimension_semantics=("arbitrary",)),
        cost_estimate=pl.CostEstimate(
            flops=2 * batches * points * wide * states,
            bytes_accessed=2 * batches * points * wide,
            transcendentals=0,
        ),
    )(batch_atom, spreads, window, occupation[None, :], jnp.transpose(harmonics, (1, 0, 2)))


def shards(coeffs, occupation, basis_on_grid, basis_map, basis_count, batch_atom, harmonics):
    batches, points, slots = basis_on_grid.shape
    owned = coeffs.shape[0]
    owners = lax.axis_size("row")
    wide = owners * WIN
    if wide == owned:
        outgoing = coeffs
    else:
        target = lax.broadcasted_iota(jnp.int32, (owners, WIN), 0)
        offset = lax.broadcasted_iota(jnp.int32, (owners, WIN), 1)
        outgoing = jnp.take(coeffs, jnp.mod(target * WIN + offset, owned).reshape(-1), axis=0)
    window = lax.all_to_all(outgoing, "row", split_axis=0, concat_axis=0, tiled=True)
    start = jnp.mod(lax.axis_index("row") * WIN, owned)
    source = basis_map // owned
    within = jnp.mod(basis_map % owned - start, owned)
    local_ids = source * WIN + within
    slot_ids = lax.broadcasted_iota(jnp.int32, (batches, slots), 1)
    local_ids = jnp.where(slot_ids < basis_count[:, None], local_ids, -1)
    spreads = spread(local_ids, basis_on_grid, wide)
    cols = lax.axis_size("col")
    parts = harmonics.shape[1]
    packed = densities(batch_atom, spreads, window, occupation, harmonics, cols)
    summed = jnp.sum(lax.all_to_all(packed, "col", split_axis=0, concat_axis=0, tiled=True), axis=0)
    density = summed[:batches]
    mine = jnp.broadcast_to(summed[None, batches:], (owners,) + summed[batches:].shape)
    gathered = lax.all_to_all(mine, "row", split_axis=0, concat_axis=0, tiled=True)
    moments = jnp.sum(gathered, axis=0)[:parts, :NATOM].T
    return (density, moments)


def solution(mesh):
    placed = (
        P("row", "col"),
        P("col"),
        P("row", None, None),
        P("row", None),
        P("row"),
        P("row"),
        P("row", None, None),
    )
    return jax.shard_map(
        shards, mesh=mesh, in_specs=placed, out_specs=(P("row", "col"), P()), check_vma=False
    )
```

```python
import jax
import jax.numpy as jnp
from jax import lax
from jax.experimental import pallas as pl
from jax.experimental.pallas import tpu as pltpu
from jax.sharding import PartitionSpec as P

WIN = 96
NATOM = 64


GROUP = 8


def spread_kernel(ids_ref, values_ref, out_ref):
    per, points, wide = out_ref.shape
    slots = ids_ref.shape[2]
    columns = lax.broadcasted_iota(jnp.int32, (slots, wide), 1)
    ids = jnp.concatenate([ids_ref[0]] * (8 // per), axis=0).T
    for j in range(per):
        place = jnp.where(columns == ids[:, j:j + 1], 1.0, 0.0).astype(jnp.bfloat16)
        out = jnp.dot(values_ref[j], place, preferred_element_type=jnp.float32)
        out_ref[j] = out.astype(jnp.bfloat16)


def spread(ids, values, wide):
    batches, points, slots = values.shape
    per = next(n for n in (4, 2, 1) if batches % n == 0 and n * wide <= 4096)
    ids = ids.reshape(batches // per, per, slots)
    return pl.pallas_call(
        spread_kernel,
        grid=(batches // per,),
        in_specs=[
            pl.BlockSpec((1, per, slots), lambda b: (b, 0, 0)),
            pl.BlockSpec((per, points, slots), lambda b: (b, 0, 0)),
        ],
        out_specs=pl.BlockSpec((per, points, wide), lambda b: (b, 0, 0)),
        out_shape=jax.ShapeDtypeStruct((batches, points, wide), jnp.bfloat16),
        compiler_params=pltpu.CompilerParams(dimension_semantics=("arbitrary",)),
        cost_estimate=pl.CostEstimate(
            flops=2 * batches * points * slots * wide,
            bytes_accessed=2 * batches * points * (slots + wide),
            transcendentals=0,
        ),
    )(ids, values)


def density_kernel(atom_ref, spread_ref, window_ref, occ_ref, harm_ref, out_ref, mom, rows):
    per = spread_ref.shape[0]
    _, points, wide = spread_ref.shape
    states = window_ref.shape[1]
    cols, _, share = out_ref.shape
    parts = harm_ref.shape[0]
    i = pl.program_id(0)
    first = pl.multiple_of(i * per, per)
    inner = lax.rem(first, GROUP)

    @pl.when(i == 0)
    def _():
        mom[...] = jnp.zeros_like(mom)

    step = min(256, states)
    lanes = min(128, step)
    pair = min(2, per)
    for j in range(0, per, pair):
        values = spread_ref[j:j + pair].reshape(pair * points, wide)
        total = jnp.zeros((pair * points, lanes), jnp.float32)
        for start in range(0, states, step):
            orbital = jnp.dot(
                values, window_ref[:, start:start + step], preferred_element_type=jnp.float32
            )
            scaled = orbital * orbital * occ_ref[:, start:start + step]
            for lane in range(0, step, lanes):
                total = total + scaled[:, lane:lane + lanes]
        for k in range(pair):
            piece = total[k * points:(k + 1) * points].T
            rows[pl.ds(inner + j + k, 1), :] = jnp.sum(piece, axis=0, keepdims=True)

    @pl.when(inner + per == GROUP)
    def _():
        base = pl.multiple_of(first + per - GROUP, GROUP)
        density = rows[...]
        for c in range(cols):
            out_ref[c, pl.ds(base, GROUP), :] = density[:, c * share:(c + 1) * share]
        local = jnp.sum(harm_ref[...] * density[None], axis=2, keepdims=True)
        spots = lax.broadcasted_iota(jnp.int32, (GROUP, NATOM), 0)
        atoms = jnp.zeros((GROUP, NATOM), jnp.int32)
        for k in range(GROUP):
            atoms = jnp.where(spots == k, atom_ref[base + k], atoms)
        lanes_of = lax.broadcasted_iota(jnp.int32, (GROUP, NATOM), 1)
        member = jnp.where(atoms == lanes_of, 1.0, 0.0)
        mom[...] += local * member[None]

    @pl.when(i == pl.num_programs(0) - 1)
    def _():
        done = jnp.sum(mom[...], axis=1)
        batches = pl.num_programs(0) * per
        for c in range(cols):
            out_ref[c, pl.ds(batches, parts), :NATOM] = done


def densities(batch_atom, spreads, window, occupation, harmonics, cols):
    batches, points, wide = spreads.shape
    states = window.shape[1]
    parts = harmonics.shape[1]
    share = points // cols
    per = GROUP if wide <= 1024 else 2
    height = batches + -(-parts // GROUP) * GROUP
    ratio = GROUP // per
    return pl.pallas_call(
        density_kernel,
        grid_spec=pltpu.PrefetchScalarGridSpec(
            num_scalar_prefetch=1,
            grid=(batches // per,),
            in_specs=[
                pl.BlockSpec((per, points, wide), lambda b, a: (b, 0, 0)),
                pl.BlockSpec((wide, states), lambda b, a: (0, 0)),
                pl.BlockSpec((1, states), lambda b, a: (0, 0)),
                pl.BlockSpec((parts, GROUP, points), lambda b, a: (0, b // ratio, 0)),
            ],
            out_specs=pl.BlockSpec((cols, height, share), lambda b, a: (0, 0, 0)),
            scratch_shapes=[
                pltpu.VMEM((parts, GROUP, NATOM), jnp.float32),
                pltpu.VMEM((GROUP, points), jnp.float32),
            ],
        ),
        out_shape=jax.ShapeDtypeStruct((cols, height, share), jnp.float32),
        compiler_params=pltpu.CompilerParams(dimension_semantics=("arbitrary",)),
        cost_estimate=pl.CostEstimate(
            flops=2 * batches * points * wide * states,
            bytes_accessed=2 * batches * points * wide,
            transcendentals=0,
        ),
    )(batch_atom, spreads, window, occupation[None, :], jnp.transpose(harmonics, (1, 0, 2)))


def shards(coeffs, occupation, basis_on_grid, basis_map, basis_count, batch_atom, harmonics):
    batches, points, slots = basis_on_grid.shape
    owned = coeffs.shape[0]
    owners = lax.axis_size("row")
    wide = owners * WIN
    if wide == owned:
        outgoing = coeffs
    else:
        target = lax.broadcasted_iota(jnp.int32, (owners, WIN), 0)
        offset = lax.broadcasted_iota(jnp.int32, (owners, WIN), 1)
        outgoing = jnp.take(coeffs, jnp.mod(target * WIN + offset, owned).reshape(-1), axis=0)
    window = lax.all_to_all(outgoing, "row", split_axis=0, concat_axis=0, tiled=True)
    start = jnp.mod(lax.axis_index("row") * WIN, owned)
    source = basis_map // owned
    within = jnp.mod(basis_map % owned - start, owned)
    local_ids = source * WIN + within
    slot_ids = lax.broadcasted_iota(jnp.int32, (batches, slots), 1)
    local_ids = jnp.where(slot_ids < basis_count[:, None], local_ids, -1)
    spreads = spread(local_ids, basis_on_grid, wide)
    cols = lax.axis_size("col")
    parts = harmonics.shape[1]
    packed = densities(batch_atom, spreads, window, occupation, harmonics, cols)
    here = lax.axis_index("col")
    summed = lax.dynamic_index_in_dim(packed, here, 0, keepdims=False)
    for k in range(1, cols):
        piece = lax.dynamic_index_in_dim(packed, jnp.mod(here + k, cols), 0, keepdims=False)
        summed = summed + lax.ppermute(piece, "col", [(c, (c + k) % cols) for c in range(cols)])
    density = summed[:batches]
    mine = summed[batches:]
    total = mine
    for k in range(1, owners):
        total = total + lax.ppermute(mine, "row", [(r, (r + k) % owners) for r in range(owners)])
    moments = total[:parts, :NATOM].T
    return (density, moments)


def solution(mesh):
    placed = (
        P("row", "col"),
        P("col"),
        P("row", None, None),
        P("row", None),
        P("row"),
        P("row"),
        P("row", None, None),
    )
    return jax.shard_map(
        shards, mesh=mesh, in_specs=placed, out_specs=(P("row", "col"), P()), check_vma=False
    )
```

```python
import jax
import jax.numpy as jnp
from jax import lax
from jax.experimental import pallas as pl
from jax.experimental.pallas import tpu as pltpu
from jax.sharding import PartitionSpec as P

WIN = 96
NATOM = 64


GROUP = 8


def spread_kernel(ids_ref, values_ref, out_ref):
    per, points, wide = out_ref.shape
    slots = ids_ref.shape[2]
    columns = lax.broadcasted_iota(jnp.int32, (slots, wide), 1)
    ids = jnp.concatenate([ids_ref[0]] * (8 // per), axis=0).T
    for j in range(per):
        place = jnp.where(columns == ids[:, j:j + 1], 1.0, 0.0).astype(jnp.bfloat16)
        out = jnp.dot(values_ref[j], place, preferred_element_type=jnp.float32)
        out_ref[j] = out.astype(jnp.bfloat16)


def spread(ids, values, wide):
    batches, points, slots = values.shape
    per = next(n for n in (4, 2, 1) if batches % n == 0 and n * wide <= 4096)
    ids = ids.reshape(batches // per, per, slots)
    return pl.pallas_call(
        spread_kernel,
        grid=(batches // per,),
        in_specs=[
            pl.BlockSpec((1, per, slots), lambda b: (b, 0, 0)),
            pl.BlockSpec((per, points, slots), lambda b: (b, 0, 0)),
        ],
        out_specs=pl.BlockSpec((per, points, wide), lambda b: (b, 0, 0)),
        out_shape=jax.ShapeDtypeStruct((batches, points, wide), jnp.bfloat16),
        compiler_params=pltpu.CompilerParams(dimension_semantics=("arbitrary",)),
        cost_estimate=pl.CostEstimate(
            flops=2 * batches * points * slots * wide,
            bytes_accessed=2 * batches * points * (slots + wide),
            transcendentals=0,
        ),
    )(ids, values)


def density_kernel(atom_ref, spread_ref, window_ref, occ_ref, harm_ref, out_ref, mom, rows):
    per = spread_ref.shape[0]
    _, points, wide = spread_ref.shape
    states = window_ref.shape[1]
    cols, _, share = out_ref.shape
    parts = harm_ref.shape[0]
    i = pl.program_id(0)
    first = pl.multiple_of(i * per, per)
    inner = lax.rem(first, GROUP)

    @pl.when(i == 0)
    def _():
        mom[...] = jnp.zeros_like(mom)

    step = min(256, states)
    lanes = min(128, step)
    pair = 1
    for j in range(0, per, pair):
        values = spread_ref[j:j + pair].reshape(pair * points, wide)
        total = jnp.zeros((pair * points, lanes), jnp.float32)
        for start in range(0, states, step):
            orbital = jnp.dot(
                values, window_ref[:, start:start + step], preferred_element_type=jnp.float32
            )
            scaled = orbital * orbital * occ_ref[:, start:start + step]
            for lane in range(0, step, lanes):
                total = total + scaled[:, lane:lane + lanes]
        for k in range(pair):
            piece = total[k * points:(k + 1) * points].T
            rows[pl.ds(inner + j + k, 1), :] = jnp.sum(piece, axis=0, keepdims=True)

    @pl.when(inner + per == GROUP)
    def _():
        base = pl.multiple_of(first + per - GROUP, GROUP)
        density = rows[...]
        for c in range(cols):
            out_ref[c, pl.ds(base, GROUP), :] = density[:, c * share:(c + 1) * share]
        local = jnp.sum(harm_ref[...] * density[None], axis=2, keepdims=True)
        spots = lax.broadcasted_iota(jnp.int32, (GROUP, NATOM), 0)
        atoms = jnp.zeros((GROUP, NATOM), jnp.int32)
        for k in range(GROUP):
            atoms = jnp.where(spots == k, atom_ref[base + k], atoms)
        lanes_of = lax.broadcasted_iota(jnp.int32, (GROUP, NATOM), 1)
        member = jnp.where(atoms == lanes_of, 1.0, 0.0)
        mom[...] += local * member[None]

    @pl.when(i == pl.num_programs(0) - 1)
    def _():
        done = jnp.sum(mom[...], axis=1)
        batches = pl.num_programs(0) * per
        for c in range(cols):
            out_ref[c, pl.ds(batches, parts), :NATOM] = done


def densities(batch_atom, spreads, window, occupation, harmonics, cols):
    batches, points, wide = spreads.shape
    states = window.shape[1]
    parts = harmonics.shape[1]
    share = points // cols
    per = GROUP if wide <= 1024 else 2
    height = batches + -(-parts // GROUP) * GROUP
    ratio = GROUP // per
    return pl.pallas_call(
        density_kernel,
        grid_spec=pltpu.PrefetchScalarGridSpec(
            num_scalar_prefetch=1,
            grid=(batches // per,),
            in_specs=[
                pl.BlockSpec((per, points, wide), lambda b, a: (b, 0, 0)),
                pl.BlockSpec((wide, states), lambda b, a: (0, 0)),
                pl.BlockSpec((1, states), lambda b, a: (0, 0)),
                pl.BlockSpec((parts, GROUP, points), lambda b, a: (0, b // ratio, 0)),
            ],
            out_specs=pl.BlockSpec((cols, height, share), lambda b, a: (0, 0, 0)),
            scratch_shapes=[
                pltpu.VMEM((parts, GROUP, NATOM), jnp.float32),
                pltpu.VMEM((GROUP, points), jnp.float32),
            ],
        ),
        out_shape=jax.ShapeDtypeStruct((cols, height, share), jnp.float32),
        compiler_params=pltpu.CompilerParams(dimension_semantics=("arbitrary",)),
        cost_estimate=pl.CostEstimate(
            flops=2 * batches * points * wide * states,
            bytes_accessed=2 * batches * points * wide,
            transcendentals=0,
        ),
    )(batch_atom, spreads, window, occupation[None, :], jnp.transpose(harmonics, (1, 0, 2)))


def shards(coeffs, occupation, basis_on_grid, basis_map, basis_count, batch_atom, harmonics):
    batches, points, slots = basis_on_grid.shape
    owned = coeffs.shape[0]
    owners = lax.axis_size("row")
    wide = owners * WIN
    if wide == owned:
        outgoing = coeffs
    else:
        target = lax.broadcasted_iota(jnp.int32, (owners, WIN), 0)
        offset = lax.broadcasted_iota(jnp.int32, (owners, WIN), 1)
        outgoing = jnp.take(coeffs, jnp.mod(target * WIN + offset, owned).reshape(-1), axis=0)
    window = lax.all_to_all(outgoing, "row", split_axis=0, concat_axis=0, tiled=True)
    start = jnp.mod(lax.axis_index("row") * WIN, owned)
    source = basis_map // owned
    within = jnp.mod(basis_map % owned - start, owned)
    local_ids = source * WIN + within
    slot_ids = lax.broadcasted_iota(jnp.int32, (batches, slots), 1)
    local_ids = jnp.where(slot_ids < basis_count[:, None], local_ids, -1)
    spreads = spread(local_ids, basis_on_grid, wide)
    cols = lax.axis_size("col")
    parts = harmonics.shape[1]
    packed = densities(batch_atom, spreads, window, occupation, harmonics, cols)
    here = lax.axis_index("col")
    summed = lax.dynamic_index_in_dim(packed, here, 0, keepdims=False)
    for k in range(1, cols):
        piece = lax.dynamic_index_in_dim(packed, jnp.mod(here + k, cols), 0, keepdims=False)
        summed = summed + lax.ppermute(piece, "col", [(c, (c + k) % cols) for c in range(cols)])
    density = summed[:batches]
    mine = summed[batches:]
    total = mine
    for k in range(1, owners):
        total = total + lax.ppermute(mine, "row", [(r, (r + k) % owners) for r in range(owners)])
    moments = total[:parts, :NATOM].T
    return (density, moments)


def solution(mesh):
    placed = (
        P("row", "col"),
        P("col"),
        P("row", None, None),
        P("row", None),
        P("row"),
        P("row"),
        P("row", None, None),
    )
    return jax.shard_map(
        shards, mesh=mesh, in_specs=placed, out_specs=(P("row", "col"), P()), check_vma=False
    )
```
